32 devices in a mesh: grp: 2 (over y), inp: 8 (over z, x), freq: 2 (over core).
Axes of the slice: x: 2, y: 2, z: 4, core: 2. Of those that a mesh axis runs over, the one named last changes fastest.
Arguments:
- voltages: int32 [2048, 64, 2048], P(('grp', 'inp'), 'freq'), parts along dimension 0, may hold values from -127 to 127, as said below
- coeffs: int32 [8, 2048], replicated, may hold values from -6144 to 6144, as said below
Outputs:
- visibilities: bfloat16 [1024, 2, 36, 128, 128], P(('grp', 'inp', 'freq')), parts along dimension 0
The draws below stay inside these ranges and needn't reach their ends.
There are 2 independent parts, one for each index of `grp`. The reference program is written for one: setup_inputs(seed, part) draws one part's arguments, and reference() takes and returns one part's arrays. A program takes and returns all parts, laid end to end along the dimension named above; an argument that names none is the same for every part. Nothing has to cross between parts.
Inputs may be any that keep to these rules, and one draw needn't show every extreme that they name: `voltages`: signed 8-bit samples. `coeffs`: integer coefficients.
All inputs are finite; a program needn't handle non-finite values.
Results may differ from the reference program's by a relative error of at most 0.0069.
Values may be sent and summed in bfloat16 or wider, within the bound.
A program may use at most 384 MiB of HBM per device.

```python
import math
import jax
import jax.numpy as jnp
from jax import lax

SPF = 2048
TAPS = 8
CH = 512
CH0 = 256
INPUTS = 1024
BLK = 128
NBLK = 8
FRAMES = 64


def draw_voltages(key, part):
    key_base, key_values = jax.random.split(jax.random.fold_in(key, 11))
    base = jax.random.randint(key_base, (INPUTS, 1, 1), 4, 32)
    frame = jnp.arange(FRAMES, dtype=jnp.int32)[None, :, None]
    limit = base * (FRAMES + 3 * frame) // FRAMES
    limit = jnp.broadcast_to(limit, (INPUTS, FRAMES, SPF))
    return jax.random.randint(key_values, (INPUTS, FRAMES, SPF), -limit, limit + 1).astype(jnp.int32)


def draw_coeffs(key, part):
    length = TAPS * SPF
    place = jnp.arange(length, dtype=jnp.int32)
    tent = jnp.minimum(place + 1, length - place) * 8192 // length
    tap = place // SPF
    sign = 1 - 2 * (jnp.abs(2 * tap - (TAPS - 1)) // 2 % 2)
    noise = jax.random.randint(jax.random.fold_in(key, 23), (length,), -(tent // 2), tent // 2 + 1)
    return (sign * tent + noise).reshape(TAPS, SPF).astype(jnp.int32)


def setup_inputs(seed: int = 0, part: int = 0) -> dict:
    streams_of = jax.random.split(jax.random.key(seed), 3)
    own_keys = jax.random.split(jax.random.fold_in(streams_of[2], part), 3)
    voltages = draw_voltages(jax.random.fold_in(jax.random.fold_in(streams_of[2], part), 71), part)
    coeffs = draw_coeffs(jax.random.fold_in(streams_of[2], 71), part)
    return dict(voltages=voltages, coeffs=coeffs)


def make_table():
    sample = jnp.arange(SPF, dtype=jnp.int32)[:, None]
    channel = jnp.arange(CH, dtype=jnp.int32)[None, :] + CH0
    phase = sample * channel % SPF
    angle = phase.astype(jnp.float32) * (2.0 * math.pi / SPF)
    return jnp.concatenate([jnp.cos(angle), -jnp.sin(angle)], axis=1).astype(jnp.bfloat16)

def block_pairs():
    return [(row_index, col_index) for row_index in range(NBLK) for col_index in range(row_index, NBLK)]

def reference(voltages, coeffs):
    dft_table = make_table().astype(jnp.float32)
    weights = coeffs.astype(jnp.float32)

    def front_end(samples):
        padded = jnp.pad(samples.astype(jnp.float32), ((0, 0), (TAPS - 1, 0), (0, 0)))
        summed = jnp.zeros((samples.shape[0], FRAMES, SPF), jnp.float32)
        for tap_index in range(TAPS):
            begin = TAPS - 1 - tap_index
            summed = summed + weights[tap_index] * padded[:, begin:begin + FRAMES, :]
        rounded = lax.optimization_barrier(summed.astype(jnp.bfloat16))
        filtered = rounded.astype(jnp.float32)
        spectrum = jnp.dot(filtered.reshape(-1, SPF), dft_table, precision=lax.Precision.HIGHEST, preferred_element_type=jnp.float32).reshape(-1, FRAMES, 2 * CH)
        power = lax.optimization_barrier(jnp.sum(spectrum * spectrum, axis=(1, 2))) / (FRAMES * CH)
        gains = 1.0 / jnp.sqrt(power + 1e-06)
        return (spectrum * gains[:, None, None]).astype(jnp.bfloat16)
    blocked = voltages.reshape(NBLK, BLK, FRAMES, SPF)
    scaled = lax.map(front_end, blocked).reshape(INPUTS, FRAMES, 2, CH)
    stacked = jnp.transpose(scaled, (3, 0, 2, 1)).reshape(CH, INPUTS, 2 * FRAMES)
    pairs = block_pairs()

    def correlate(operand):
        first = operand.astype(jnp.float32)
        second = jnp.concatenate([-first[:, FRAMES:], first[:, :FRAMES]], axis=1)
        real_part = jnp.dot(first, first.T, precision=lax.Precision.HIGHEST, preferred_element_type=jnp.float32)
        imag_part = jnp.dot(first, second.T, precision=lax.Precision.HIGHEST, preferred_element_type=jnp.float32)
        grams = jnp.stack([real_part, imag_part]) * (1.0 / FRAMES)
        picked = jnp.stack([grams[:, row_index * BLK:(row_index + 1) * BLK, col_index * BLK:(col_index + 1) * BLK] for row_index, col_index in pairs], axis=1)
        return picked.astype(jnp.bfloat16)
    return lax.map(correlate, stacked)
```

```python
import functools
import math

import jax
import jax.numpy as jnp
import numpy as np
from jax import lax
from jax.experimental import pallas as pl
from jax.experimental.pallas import tpu as pltpu
from jax.sharding import PartitionSpec as P

SPF = 2048
TAPS = 8
CH = 512
CH0 = 256
INPUTS = 1024
BLK = 128


def passed_along(x, axis, by):
    length = lax.axis_size(axis)
    pairs = [(i, i + by) for i in range(length) if 0 <= i + by < length]
    return lax.ppermute(x, axis, pairs)


def make_table():
    sample = jnp.arange(SPF, dtype=jnp.int32)[:, None]
    channel = jnp.arange(CH, dtype=jnp.int32)[None, :] + CH0
    phase = sample * channel % SPF
    angle = phase.astype(jnp.float32) * (2.0 * math.pi / SPF)
    return jnp.concatenate([jnp.cos(angle), -jnp.sin(angle)], axis=1).astype(jnp.bfloat16)


def plain_device(voltages, coeffs):
    inputs_here = voltages.shape[0]
    frames_here = voltages.shape[1]
    inp_count = lax.axis_size("inp")
    freq_count = lax.axis_size("freq")
    frames_all = frames_here * freq_count
    history = voltages[:, frames_here - (TAPS - 1) :, :].astype(jnp.bfloat16)
    earlier = passed_along(history, "freq", 1)
    extended = jnp.concatenate([earlier.astype(jnp.float32), voltages.astype(jnp.float32)], axis=1)
    weights = coeffs.astype(jnp.float32)
    summed = jnp.zeros((inputs_here, frames_here, SPF), jnp.float32)
    for tap_index in range(TAPS):
        begin = TAPS - 1 - tap_index
        summed = summed + weights[tap_index] * extended[:, begin : begin + frames_here, :]
    filtered = summed.astype(jnp.bfloat16).reshape(inputs_here * frames_here, SPF)
    spectrum_t = jnp.einsum("nj,rn->jr", make_table(), filtered, preferred_element_type=jnp.float32)
    spectrum_t = spectrum_t.reshape(2 * CH, inputs_here, frames_here)
    squares = jnp.sum(spectrum_t * spectrum_t, axis=(0, 2))
    power = lax.psum(squares, "freq") / (frames_all * CH)
    gains = 1.0 / jnp.sqrt(power + 1e-06)
    scaled = (spectrum_t * gains[None, :, None]).astype(jnp.bfloat16)
    scaled = scaled.reshape(2, CH, inputs_here * frames_here)
    arrived = lax.all_to_all(scaled[None], ("inp", "freq"), split_axis=2, concat_axis=0, tiled=True)
    width_here = arrived.shape[-2]
    arranged = arrived.reshape(inp_count, freq_count, 2, width_here, inputs_here, frames_here)
    arranged = jnp.transpose(arranged, (3, 0, 4, 2, 1, 5))
    stacked = arranged.reshape(width_here, INPUTS, 2 * frames_all)
    other = jnp.concatenate([-stacked[:, :, frames_all:], stacked[:, :, :frames_all]], axis=2)
    block_count = INPUTS // BLK
    scale = 1.0 / frames_all
    pieces = []
    for row_index in range(block_count):
        row_panel = stacked[:, row_index * BLK : (row_index + 1) * BLK]
        real_part = jnp.einsum(
            "cut,cmt->cum",
            row_panel,
            stacked[:, row_index * BLK :],
            preferred_element_type=jnp.float32,
        )
        imag_part = jnp.einsum(
            "cut,cmt->cum",
            row_panel,
            other[:, row_index * BLK :],
            preferred_element_type=jnp.float32,
        )
        band = jnp.stack([real_part, imag_part], axis=1) * scale
        for col_index in range(row_index, block_count):
            begin = (col_index - row_index) * BLK
            pieces.append(band[:, :, :, begin : begin + BLK])
    return jnp.stack(pieces, axis=2).astype(jnp.bfloat16)


MESH = pl.DeviceIdType.MESH
GROUP = 8
LANE = 128
HALF = 16
PLANE = 4


def table_rows(count):
    sample = np.arange(SPF, dtype=np.int32)[None, :]
    channel = np.arange(CH, dtype=np.int32)[:, None] + CH0
    angle = (sample * channel % SPF).astype(np.float32) * np.float32(2.0 * math.pi / SPF)
    both = np.stack([np.cos(angle), -np.sin(angle)])
    rows = both.reshape(2, count, CH // count, SPF).transpose(1, 0, 2, 3).reshape(2 * CH, SPF)
    return jnp.asarray(rows.astype(jnp.bfloat16))


def front_kernel(
    inp_count,
    freq_count,
    volts,
    coeffs,
    table_hbm,
    spec,
    arrived,
    powers,
    frames,
    history,
    table,
    filtered,
    spread,
    staged,
    power,
    load_sem,
    table_sem,
    hist_send,
    hist_recv,
    stage_sem,
    send_sem,
    recv_sem,
    pow_sem,
    pow_send,
    pow_recv,
):
    grp = lax.axis_index("grp")
    inp = lax.axis_index("inp")
    freq = lax.axis_index("freq")
    count = inp_count * freq_count
    me = inp * freq_count + freq
    inputs_here, frames_here, _ = volts.shape
    halves = frames_here // HALF
    taps = coeffs.shape[0]
    per_owner = spec.shape[2]
    rows = PLANE * per_owner
    planes = count // PLANE

    def where(index):
        return (grp, index // freq_count, index % freq_count)

    def load(t):
        return pltpu.make_async_copy(volts.at[:, t, :], frames.at[t], load_sem.at[t])

    half_order = list(reversed(range(halves)))
    fetch_order = []
    for half in half_order:
        for t in range(max(0, half * HALF - taps + 1), (half + 1) * HALF):
            if t not in fetch_order:
                fetch_order.append(t)
    for t in fetch_order:
        load(t).start()
    table_copy = pltpu.make_async_copy(table_hbm, table, table_sem)
    table_copy.start()

    barrier = pltpu.get_barrier_semaphore()

    def greet(step, carry):
        other = (me + step) % count
        pl.semaphore_signal(barrier, inc=1, device_id=where(other), device_id_type=MESH)
        return carry

    lax.fori_loop(1, count, greet, 0)
    power[...] = jnp.zeros_like(power)
    pl.semaphore_wait(barrier, count - 1)

    def history_copy(step):
        return pltpu.make_async_remote_copy(
            src_ref=volts.at[:, frames_here - taps + 1 + step, :],
            dst_ref=history.at[step],
            send_sem=hist_send.at[step],
            recv_sem=hist_recv.at[step],
            device_id=(grp, inp, 1),
            device_id_type=MESH,
        )

    @pl.when(freq == 0)
    def _():
        for step in range(taps - 1):
            history_copy(step).start()
        history[...] = jnp.zeros_like(history)

    loaded = set()

    def filter_group(first, base):
        def tile(index, carry):
            lanes = SPF // LANE
            row = pl.multiple_of(index // lanes * 16, 16)
            col = pl.multiple_of(index % lanes * LANE, LANE)

            def sample(t):
                if t < 0:
                    return history[taps - 1 + t, pl.ds(row, 16), pl.ds(col, LANE)].astype(jnp.float32)
                return frames[t, pl.ds(row, 16), pl.ds(col, LANE)].astype(jnp.float32)

            window = {t: sample(t) for t in range(first - taps + 1, first + GROUP)}
            weights = [coeffs[k, :, pl.ds(col, LANE)] for k in range(taps)]
            for t in range(first, first + GROUP):
                total = weights[0] * window[t]
                for k in range(1, taps):
                    total = total + weights[k] * window[t - k]
                at = pl.multiple_of((t - base) * inputs_here + row, 16)
                filtered[pl.ds(at, 16), pl.ds(col, LANE)] = total.astype(jnp.bfloat16)
            return carry

        lax.fori_loop(0, inputs_here // 16 * (SPF // LANE), tile, 0)

    def remote(half, other):
        return pltpu.make_async_remote_copy(
            src_ref=spec.at[other, half],
            dst_ref=arrived.at[me, half],
            send_sem=send_sem.at[half, other],
            recv_sem=recv_sem.at[half, me],
            device_id=where(other),
            device_id_type=MESH,
        )

    plane_here = me // PLANE
    if planes == 4:
        order = [
            (plane_here + 2) % 4,
            3 - plane_here,
            plane_here + 1 - 2 * (plane_here % 2),
            plane_here,
        ]
    else:
        order = [(plane_here + planes // 2 + step) % planes for step in range(planes)]

    frames_step = 4
    for half_number, half in enumerate(half_order):
        for first in range(half * HALF, (half + 1) * HALF, GROUP):
            for t in range(max(0, first - taps + 1), first + GROUP):
                if t not in loaded:
                    loaded.add(t)
                    load(t).wait()
            if first == 0:

                @pl.when(freq != 0)
                def _():
                    for step in range(taps - 1):
                        history_copy(step).wait_recv()

            filter_group(first, half * HALF)
        if half_number == 0:
            table_copy.wait()
        for plane in order:

            def transform(step, carry):
                lines = table[pl.ds(pl.multiple_of(plane * rows, rows), rows), :]
                at = pl.multiple_of(step * (frames_step * inputs_here), frames_step * inputs_here)
                chunk = filtered[pl.ds(at, frames_step * inputs_here), :]
                product = lax.dot_general(
                    lines, chunk, (((1,), (1,)), ((), ())), preferred_element_type=jnp.float32
                )
                total = jnp.zeros((8, LANE), jnp.float32)
                for t in range(frames_step):
                    piece = product[:, t * LANE : (t + 1) * LANE]
                    spread[pl.ds(step * frames_step + t, rows, stride=HALF), :] = piece
                    total = total + jnp.sum((piece * piece).reshape(rows // 8, 8, LANE), axis=0)
                power[...] += total
                return carry

            lax.fori_loop(0, HALF // frames_step, transform, 0)

            def convert(step, carry):
                at = pl.multiple_of(step * (per_owner * HALF), per_owner * HALF)
                block = spread[pl.ds(at, per_owner * HALF), :].astype(jnp.bfloat16)
                staged[step] = block.reshape(per_owner, HALF, LANE)
                return carry

            lax.fori_loop(0, PLANE, convert, 0)

            def put_away(step, start):
                owner = plane * PLANE + step
                away = pltpu.make_async_copy(staged.at[step], spec.at[owner, half], stage_sem.at[step])
                here = pltpu.make_async_copy(staged.at[step], arrived.at[owner, half], stage_sem.at[step])

                @pl.when(owner != me)
                def _():
                    if start:
                        away.start()
                    else:
                        away.wait()
                        remote(half, owner).start()

                @pl.when(owner == me)
                def _():
                    if start:
                        here.start()
                    else:
                        here.wait()

            for step in range(PLANE):
                put_away(step, True)
            for step in range(PLANE):
                put_away(step, False)

    power_copy = pltpu.make_async_copy(power, powers.at[me], pow_sem)
    power_copy.start()
    power_copy.wait()

    def power_remote(other):
        return pltpu.make_async_remote_copy(
            src_ref=powers.at[me],
            dst_ref=powers.at[me],
            send_sem=pow_send.at[other],
            recv_sem=pow_recv.at[me],
            device_id=where(other),
            device_id_type=MESH,
        )

    def send_power(step, carry):
        power_remote((me + step) % count).start()
        return carry

    lax.fori_loop(1, count, send_power, 0)

    @pl.when(freq == 0)
    def _():
        for step in range(taps - 1):
            history_copy(step).wait_send()

    def finish(step, carry):
        other = (me + step) % count
        for half in range(halves):
            remote(half, other).wait_send()
            pltpu.make_async_remote_copy(
                src_ref=spec.at[other, half],
                dst_ref=arrived.at[other, half],
                send_sem=send_sem.at[half, other],
                recv_sem=recv_sem.at[half, other],
                device_id=where(other),
                device_id_type=MESH,
            ).wait_recv()
        power_remote(other).wait_send()
        pltpu.make_async_remote_copy(
            src_ref=powers.at[other],
            dst_ref=powers.at[other],
            send_sem=pow_send.at[other],
            recv_sem=pow_recv.at[other],
            device_id=where(other),
            device_id_type=MESH,
        ).wait_recv()
        return carry

    lax.fori_loop(1, count, finish, 0)


def front(voltages, coeffs, inp_count, freq_count):
    inputs_here, frames_here, _ = voltages.shape
    taps = coeffs.shape[0]
    count = inp_count * freq_count
    per_owner = 2 * CH // count
    halves = frames_here // HALF
    wide = jnp.broadcast_to(coeffs.astype(jnp.float32)[:, None, :], (taps, 16, SPF))
    anywhere = pl.BlockSpec(memory_space=pl.ANY)
    blocks = jax.ShapeDtypeStruct((count, halves, per_owner, HALF, LANE), jnp.bfloat16)
    _, arrived, powers = pl.pallas_call(
        functools.partial(front_kernel, inp_count, freq_count),
        out_shape=(blocks, blocks, jax.ShapeDtypeStruct((count, 8, LANE), jnp.float32)),
        in_specs=[anywhere, pl.BlockSpec(memory_space=pltpu.VMEM), anywhere],
        out_specs=(anywhere, anywhere, anywhere),
        scratch_shapes=[
            pltpu.VMEM((frames_here, inputs_here, SPF), jnp.int32),
            pltpu.VMEM((taps - 1, inputs_here, SPF), jnp.int32),
            pltpu.VMEM((2 * CH, SPF), jnp.bfloat16),
            pltpu.VMEM((HALF * inputs_here, SPF), jnp.bfloat16),
            pltpu.VMEM((PLANE * per_owner * HALF, LANE), jnp.float32),
            pltpu.VMEM((PLANE, per_owner, HALF, LANE), jnp.bfloat16),
            pltpu.VMEM((8, LANE), jnp.float32),
            pltpu.SemaphoreType.DMA((frames_here,)),
            pltpu.SemaphoreType.DMA,
            pltpu.SemaphoreType.DMA((taps - 1,)),
            pltpu.SemaphoreType.DMA((taps - 1,)),
            pltpu.SemaphoreType.DMA((PLANE,)),
            pltpu.SemaphoreType.DMA((halves, count)),
            pltpu.SemaphoreType.DMA((halves, count)),
            pltpu.SemaphoreType.DMA,
            pltpu.SemaphoreType.DMA((count,)),
            pltpu.SemaphoreType.DMA((count,)),
        ],
        compiler_params=pltpu.CompilerParams(
            collective_id=0, has_side_effects=True, vmem_limit_bytes=67043328
        ),
        name="front",
    )(voltages, wide, table_rows(count))
    return arrived, powers


def correlate_kernel(block, gain_row, gain_col, out, turned):
    panels, freq_count, halves = block.shape[:3]
    order = [(f, h) for f in range(freq_count) for h in range(halves)]
    straight, crossed = [], []
    for panel in range(panels):
        real = jnp.concatenate([block[panel, f, h, 0, 0] for f, h in order], axis=0)
        imag = jnp.concatenate([block[panel, f, h, 1, 0] for f, h in order], axis=0)
        both = jnp.concatenate([real, imag], axis=0)
        straight.append(both)
        crossed.append(jnp.concatenate([-imag, real], axis=0))
        turned[panel * BLK : (panel + 1) * BLK, :] = both.T
    for col in range(panels):
        weights = jnp.concatenate([straight[col], crossed[col]], axis=1)
        product = jnp.dot(
            turned[: (col + 1) * BLK, :], weights, preferred_element_type=jnp.float32
        )
        for row in range(col + 1):
            pair = row * panels - row * (row - 1) // 2 + col - row
            gain = gain_col[row * BLK : (row + 1) * BLK, :] * gain_row[col : col + 1, :]
            part = product[row * BLK : (row + 1) * BLK]
            out[0, 0, pair] = (part[:, :BLK] * gain).astype(jnp.bfloat16)
            out[0, 1, pair] = (part[:, BLK:] * gain).astype(jnp.bfloat16)


def correlate(arrived, gains, inp_count, freq_count, frames_all):
    count, halves, per_owner, _, _ = arrived.shape
    width = per_owner // 2
    pairs = inp_count * (inp_count + 1) // 2
    blocks = arrived.reshape(inp_count, freq_count, halves, 2, width, HALF, LANE)
    column = jnp.broadcast_to((gains * (1.0 / frames_all)).reshape(-1, 1), (inp_count * BLK, BLK))
    return pl.pallas_call(
        correlate_kernel,
        grid=(width,),
        out_shape=jax.ShapeDtypeStruct((width, 2, pairs, BLK, BLK), jnp.bfloat16),
        in_specs=[
            pl.BlockSpec(
                (inp_count, freq_count, halves, 2, 1, HALF, LANE), lambda c: (0, 0, 0, 0, c, 0, 0)
            ),
            pl.BlockSpec((inp_count, BLK), lambda c: (0, 0)),
            pl.BlockSpec((inp_count * BLK, BLK), lambda c: (0, 0)),
        ],
        out_specs=pl.BlockSpec((1, 2, pairs, BLK, BLK), lambda c: (c, 0, 0, 0, 0)),
        scratch_shapes=[pltpu.VMEM((inp_count * BLK, 2 * frames_all), jnp.bfloat16)],
        compiler_params=pltpu.CompilerParams(vmem_limit_bytes=48 * 1024 * 1024),
        name="correlate",
    )(blocks, gains, column)


def per_device(voltages, coeffs):
    inputs_here, frames_here, _ = voltages.shape
    inp_count = lax.axis_size("inp")
    freq_count = lax.axis_size("freq")
    count = inp_count * freq_count
    frames_all = frames_here * freq_count
    fits = (
        inputs_here == BLK
        and freq_count == 2
        and frames_here % HALF == 0
        and count % PLANE == 0
        and CH % count == 0
        and 2 * frames_all % LANE == 0
    )
    if not fits:
        return plain_device(voltages, coeffs)
    arrived, powers = front(voltages, coeffs, inp_count, freq_count)
    power = jnp.sum(powers.reshape(inp_count, freq_count * 8, LANE), axis=1) / (frames_all * CH)
    gains = 1.0 / jnp.sqrt(power + 1e-06)
    return correlate(arrived, gains, inp_count, freq_count, frames_all)


def solution(mesh):
    in_specs = (P(("grp", "inp"), "freq", None), P())
    out_specs = P(("grp", "inp", "freq"), None, None, None, None)
    return jax.shard_map(
        per_device, mesh=mesh, in_specs=in_specs, out_specs=out_specs, check_vma=False
    )
```
